32 devices in a mesh: heads: 4 (over y, x), seq: 8 (over z, core).
Axes of the slice: x: 2, y: 2, z: 4, core: 2. Of those that a mesh axis runs over, the one named last changes fastest.
Arguments:
- local_qkv: bfloat16 [3, 4096, 2048], P(None, 'seq', 'heads'), may hold values from -8 to 8
- routed_qkv: bfloat16 [3, 4096, 2048], P(None, 'seq', 'heads'), may hold values from -8 to 8
- clusters: int32 [16, 4096], P('heads', 'seq'), may hold values from 0 to 127, as said below
- wo_local: bfloat16 [2048, 4096], P('heads'), may hold values from -0.5 to 0.5
- wo_routed: bfloat16 [2048, 4096], P('heads'), may hold values from -0.5 to 0.5
Outputs:
- layer_out: bfloat16 [4096, 4096], P('seq', 'heads')
The draws below stay inside these ranges and needn't reach their ends.
Inputs may be any that keep to these rules, and one draw needn't show every extreme that they name: `clusters`: in every routed head, no cluster holds more than 8 of the 512 tokens of one aligned block of tokens; in every head and block some cluster holds exactly 8 of them.
All inputs are finite; a program needn't handle non-finite values.
Results may differ from the reference program's by a relative error of at most 0.009.
Values may be sent and summed in bfloat16 or wider, within the bound.
A program may use at most 128 MiB of HBM per device.

```python
import jax
import jax.numpy as jnp
from jax import lax

D = 4096
DH = 128
LOCAL_HEADS = 16
ROUTED_HEADS = 16
TOK_DEV = 512
WINDOW = 512
NCLUST = 128
MOST = 8
TOKENS = 4096
N_HEADS = 4
N_SEQ = 8


def cluster_table(base_key):
    block_count = TOKENS // TOK_DEV
    slot_count = NCLUST * MOST
    order_key, noise_key, shuffle_key = jax.random.split(base_key, 3)
    priority = jax.vmap(lambda k: jax.random.permutation(k, NCLUST))(jax.random.split(order_key, ROUTED_HEADS)).astype(jnp.int32)
    labels = jnp.arange(slot_count, dtype=jnp.int32) // MOST
    ranked = priority[:, labels]
    noise = jax.random.randint(noise_key, (ROUTED_HEADS, block_count, slot_count), 0, NCLUST)
    scored = ranked[:, None, :] * 2 + noise
    scored = jnp.where(ranked[:, None, :] == 0, -1, scored)
    scored = scored * 16384 + jnp.arange(slot_count, dtype=jnp.int32)
    picked = jnp.argsort(scored, axis=-1)[..., :TOK_DEV]
    chosen = labels[picked]
    shuffles = jax.vmap(lambda k: jax.random.permutation(k, TOK_DEV))(jax.random.split(shuffle_key, ROUTED_HEADS * block_count))
    shuffles = shuffles.reshape(ROUTED_HEADS, block_count, TOK_DEV)
    chosen = jnp.take_along_axis(chosen, shuffles, axis=-1)
    return chosen.reshape(ROUTED_HEADS, TOKENS).astype(jnp.int32)


def float_base(base_key, shape):
    return jnp.clip(jax.random.normal(base_key, shape, jnp.float32), -4.5, 4.5)


def draw_local_qkv(key, part):
    width = LOCAL_HEADS * DH
    base = float_base(jax.random.fold_in(key, 1), (3, TOKENS, width))
    return base.astype(jnp.bfloat16)


def draw_routed_qkv(key, part):
    width = ROUTED_HEADS * DH
    base = float_base(jax.random.fold_in(key, 2), (3, TOKENS, width))
    return base.astype(jnp.bfloat16)


def draw_clusters(key, part):
    return cluster_table(jax.random.fold_in(key, 11))


def block_levels(rng, shape, cuts, least, largest):
    gain, own = 1.0, jax.random.fold_in(rng, 6)
    for dim, shards_of in cuts:
        heights = jnp.exp(jax.random.uniform(jax.random.fold_in(own, dim), (shards_of,), jnp.float32, least / len(cuts), largest / len(cuts)))
        gain = gain * jnp.repeat(heights, shape[dim] // shards_of).reshape([-1 if axis == dim else 1 for axis in range(len(shape))])
    return gain


def centred(rng, dims, spread, most, cuts=(), kind=jnp.bfloat16):
    entries = jax.random.normal(rng, dims, jnp.float32) * spread
    if len(cuts) > 0:
        entries = block_levels(rng, dims, cuts, -0.22, 0.18) * entries
    return jnp.clip(entries, min=-most, max=most).astype(kind)


def setup_inputs(seed: int = 0) -> dict:
    streams_of = jax.random.split(jax.random.key(seed), 6)
    return {
        "local_qkv": draw_local_qkv(jax.random.fold_in(streams_of[5], 71), 0),
        "routed_qkv": draw_routed_qkv(jax.random.fold_in(streams_of[5], 71), 0),
        "clusters": draw_clusters(jax.random.fold_in(streams_of[5], 71), 0),
        "wo_local": centred(streams_of[3], (LOCAL_HEADS * DH, D), DH ** -0.5, 0.5, ((0, 4),)),
        "wo_routed": centred(streams_of[4], (ROUTED_HEADS * DH, D), DH ** -0.5, 0.5, ((0, 4),)),
    }


masked_fill = -1e30


def attend(scores, allowed, values, form):
    scores = jnp.where(allowed, scores, masked_fill)
    top_score = jnp.max(scores, axis=-1, keepdims=True)
    raised = jnp.exp(scores - top_score)
    weights = (raised / jnp.sum(raised, axis=-1, keepdims=True)).astype(jnp.bfloat16)
    weights = lax.optimization_barrier(weights)
    return jnp.einsum(form, weights.astype(jnp.float32), values.astype(jnp.float32)).astype(jnp.bfloat16)


def window_attend(qkv):
    width = qkv.shape[2]
    head_count = width // DH
    queries = qkv[0].reshape(TOKENS, head_count, DH)
    padded = jnp.concatenate([jnp.zeros((2, WINDOW, width), qkv.dtype), qkv[1:]], axis=1)

    def one_block(index):
        start = index * WINDOW
        block_q = lax.dynamic_slice_in_dim(queries, start, WINDOW, 0).astype(jnp.float32)
        block_kv = lax.dynamic_slice_in_dim(padded, start, 2 * WINDOW, 1).astype(jnp.float32)
        keys_here = block_kv[0].reshape(2 * WINDOW, head_count, DH)
        values_here = block_kv[1].reshape(2 * WINDOW, head_count, DH)
        scores = jnp.einsum("qhd,khd->hqk", block_q, keys_here) * (DH ** -0.5)
        query_at = start + jnp.arange(WINDOW, dtype=jnp.int32)
        key_at = start - WINDOW + jnp.arange(2 * WINDOW, dtype=jnp.int32)
        offset = key_at[None, :] - query_at[:, None]
        allowed = (offset <= 0) & (offset > -WINDOW) & (key_at[None, :] >= 0)
        return attend(scores, allowed[None], values_here, "hqk,khd->qhd").reshape(WINDOW, width)

    blocks = lax.map(one_block, jnp.arange(TOKENS // WINDOW, dtype=jnp.int32))
    return blocks.reshape(TOKENS, width)


def cluster_attend(qkv, table):
    head_count = table.shape[0]
    span = N_SEQ * MOST
    token_ids = jnp.arange(TOKENS, dtype=jnp.int32)

    def one_head(index):
        labels = table[index]
        order_index = jnp.argsort(labels * TOKENS + token_ids).astype(jnp.int32)
        head_rows = lax.dynamic_slice_in_dim(qkv, index * DH, DH, 2)
        sorted_rows = head_rows[:, order_index].astype(jnp.float32)
        sorted_labels = labels[order_index]
        padded_rows = jnp.concatenate([jnp.zeros((3, span, DH), jnp.float32), sorted_rows], axis=1)
        padded_labels = jnp.concatenate([jnp.full((span,), -1, jnp.int32), sorted_labels])
        padded_at = jnp.concatenate([jnp.full((span,), -1, jnp.int32), order_index])

        def one_block(block):
            start = block * span
            block_q = lax.dynamic_slice_in_dim(sorted_rows[0], start, span, 0)
            nearby = lax.dynamic_slice_in_dim(padded_rows, start, 2 * span, 1)
            query_label = lax.dynamic_slice_in_dim(sorted_labels, start, span, 0)
            query_at = lax.dynamic_slice_in_dim(order_index, start, span, 0)
            key_label = lax.dynamic_slice_in_dim(padded_labels, start, 2 * span, 0)
            key_at = lax.dynamic_slice_in_dim(padded_at, start, 2 * span, 0)
            scores = jnp.einsum("qd,kd->qk", block_q, nearby[1]) * (DH ** -0.5)
            allowed = (key_label[None, :] == query_label[:, None]) & (key_at[None, :] <= query_at[:, None])
            return attend(scores, allowed, nearby[2], "qk,kd->qd")

        outputs = lax.map(one_block, jnp.arange(TOKENS // span, dtype=jnp.int32)).reshape(TOKENS, DH)
        return jnp.zeros((TOKENS, DH), jnp.bfloat16).at[order_index].set(outputs)

    per_head = lax.map(one_head, jnp.arange(head_count, dtype=jnp.int32))
    return per_head.transpose(1, 0, 2).reshape(TOKENS, head_count * DH)


def reference(local_qkv, routed_qkv, clusters, wo_local, wo_routed):
    local_out = window_attend(local_qkv)
    routed_out = cluster_attend(routed_qkv, clusters)
    group_local = local_out.shape[1] // N_HEADS
    group_routed = routed_out.shape[1] // N_HEADS

    def one_rows(index):
        start = index * TOK_DEV
        rows_local = lax.dynamic_slice_in_dim(local_out, start, TOK_DEV, 0)
        rows_routed = lax.dynamic_slice_in_dim(routed_out, start, TOK_DEV, 0)
        total = jnp.zeros((TOK_DEV, D), jnp.float32)
        for group in range(N_HEADS):
            low_local = group * group_local
            low_routed = group * group_routed
            group_sum = jnp.dot(rows_local[:, low_local:low_local + group_local], wo_local[low_local:low_local + group_local], preferred_element_type=jnp.float32)
            group_sum = group_sum + jnp.dot(rows_routed[:, low_routed:low_routed + group_routed], wo_routed[low_routed:low_routed + group_routed], preferred_element_type=jnp.float32)
            total = total + lax.optimization_barrier(group_sum.astype(jnp.bfloat16)).astype(jnp.float32)
        return total.astype(jnp.bfloat16)

    layer_out = lax.map(one_rows, jnp.arange(TOKENS // TOK_DEV, dtype=jnp.int32))
    return layer_out.reshape(TOKENS, D)
```

```python
import functools
import math

import jax
import jax.numpy as jnp
from jax import lax
from jax.experimental import pallas as pl
from jax.experimental.pallas import tpu as pltpu
from jax.sharding import PartitionSpec as P

DH = 128
WINDOW = 512
MASKED = -1e30
SCALE2 = math.log2(math.e) / math.sqrt(DH)
VMEM_LIMIT = 56 << 20

NT = (((1,), (1,)), ((), ()))
MESH = pl.DeviceIdType.MESH


def vmem():
    return pl.BlockSpec(memory_space=pltpu.VMEM)


def dot_nt(a, b):
    return lax.dot_general(a, b, NT, preferred_element_type=jnp.float32)


def dot(a, b):
    return jnp.dot(a, b, preferred_element_type=jnp.float32)


def window_kernel(first_ref, own_ref, prev_ref, out_ref):
    tok_count, width = out_ref.shape
    rows = min(256, tok_count)
    span = rows + WINDOW
    is_first = first_ref[0] == 0
    for i in range(tok_count // rows):
        r = lax.broadcasted_iota(jnp.int32, (rows, span), 0)
        c = lax.broadcasted_iota(jnp.int32, (rows, span), 1)
        from_prev = WINDOW - i * rows
        lowest = jnp.where(is_first, from_prev, 0)
        allowed = (c > r) & (c <= r + WINDOW) & (c >= lowest)
        for h in range(width // DH):
            cols = slice(h * DH, (h + 1) * DH)
            q = own_ref[0, i * rows:(i + 1) * rows, cols]
            k = jnp.concatenate(
                [prev_ref[0, i * rows:, cols], own_ref[1, :(i + 1) * rows, cols]], axis=0)
            v = jnp.concatenate(
                [prev_ref[1, i * rows:, cols], own_ref[2, :(i + 1) * rows, cols]], axis=0)
            s = jnp.where(allowed, dot_nt(q, k), MASKED)
            top = jnp.max(s, axis=-1, keepdims=True)
            p = jnp.exp2((s - top) * SCALE2)
            total = jnp.sum(p, axis=-1, keepdims=True)
            o = dot(p.astype(jnp.bfloat16), v) / total
            out_ref[i * rows:(i + 1) * rows, cols] = o.astype(jnp.bfloat16)


def window_part(local_qkv):
    tok_count = local_qkv.shape[1]
    width = local_qkv.shape[2]
    n = lax.axis_size("seq")
    prev = lax.ppermute(local_qkv[1:], "seq", [(i, i + 1) for i in range(n - 1)])
    where_at = lax.axis_index("seq").astype(jnp.int32).reshape(1)
    return pl.pallas_call(
        window_kernel,
        out_shape=jax.ShapeDtypeStruct((tok_count, width), jnp.bfloat16),
        in_specs=[pl.BlockSpec(memory_space=pltpu.SMEM), vmem(), vmem()],
        out_specs=vmem(),
        cost_estimate=pl.CostEstimate(
            flops=4 * tok_count * 768 * width, bytes_accessed=6 << 20, transcendentals=2 << 20),
        compiler_params=pltpu.CompilerParams(vmem_limit_bytes=VMEM_LIMIT),
    )(where_at, local_qkv, prev)


def cluster_kernel(pair, r_ref, kv_ref, cq_ref, ck_ref, qpos_ref, kpos_ref, out_ref):
    n, rows, _ = out_ref.shape

    def keys(j, which):
        if pair:
            return jnp.concatenate([r_ref[j, 1 + which], kv_ref[j, which]], axis=0)
        return jnp.concatenate([kv_ref[p, j, which] for p in range(kv_ref.shape[0])], axis=0)

    def one_block(b, _):
        q = r_ref[b, 0]
        cq = cq_ref[b]

        def scores(j):
            return dot_nt(q, keys(j, 0)), cq == ck_ref[j]

        s, same = scores(b)
        s = jnp.where(same & (kpos_ref[...] <= qpos_ref[...]), s, MASKED)
        top = jnp.max(s, axis=-1, keepdims=True)
        p = jnp.exp2((s - top) * SCALE2)
        total = jnp.sum(p, axis=-1, keepdims=True)
        acc = dot(p.astype(jnp.bfloat16), keys(b, 1))

        def one_chunk(j, carry):
            top, total, acc = carry
            s, same = scores(j)
            s = jnp.where(same, s, MASKED)
            new_top = jnp.maximum(top, jnp.max(s, axis=-1, keepdims=True))
            fade = jnp.exp2((top - new_top) * SCALE2)
            p = jnp.exp2((s - new_top) * SCALE2)
            total = fade * total + jnp.sum(p, axis=-1, keepdims=True)
            acc = fade * acc + dot(p.astype(jnp.bfloat16), keys(j, 1))
            return new_top, total, acc

        top, total, acc = lax.fori_loop(0, b, one_chunk, (top, total, acc))
        out_ref[b] = (acc / total).astype(jnp.bfloat16)
        return 0

    lax.fori_loop(0, n, one_block, 0)


def routed_part(routed_qkv, clusters):
    tok_count = routed_qkv.shape[1]
    head_count = clusters.shape[0]
    n = lax.axis_size("seq")
    me = lax.axis_index("seq")
    group = n // head_count
    rows = tok_count // group
    part = me % group
    table = lax.all_gather(clusters, "seq")
    send = routed_qkv.reshape(3, group, rows, head_count, DH).transpose(3, 1, 0, 2, 4)
    send = send.reshape(n, 3, rows, DH)
    got = lax.all_to_all(send, "seq", split_axis=0, concat_axis=0, tiled=True)
    mine = lax.dynamic_index_in_dim(table, me // group, 1, keepdims=False)
    by_part = mine.reshape(n, group, rows)
    cq = lax.dynamic_index_in_dim(by_part, part, 1, keepdims=False)[:, :, None]
    at = jnp.arange(tok_count, dtype=jnp.int32).reshape(group, rows)
    qpos = lax.dynamic_index_in_dim(at, part, 0, keepdims=False)[:, None]
    pair = group == 2
    if pair:
        other = lax.ppermute(got[:, 1:], "seq", [(i, i + 1 - 2 * (i % 2)) for i in range(n)])
        ck = jnp.where(part == 0, by_part, by_part[:, ::-1])
        kpos = jnp.where(part == 0, at, at[::-1])
    else:
        groups = [[h * group + p for p in range(group)] for h in range(head_count)]
        other = lax.all_gather(got[:, 1:], "seq", axis_index_groups=groups)
        ck, kpos = by_part, at
    out = pl.pallas_call(
        functools.partial(cluster_kernel, pair),
        out_shape=jax.ShapeDtypeStruct((n, rows, DH), jnp.bfloat16),
        in_specs=[vmem()] * 6,
        out_specs=vmem(),
        compiler_params=pltpu.CompilerParams(vmem_limit_bytes=VMEM_LIMIT),
    )(got, other, cq, ck.reshape(n, 1, tok_count), qpos, kpos.reshape(1, tok_count))
    back = lax.all_to_all(out, "seq", split_axis=0, concat_axis=0, tiled=True)
    return back.reshape(head_count, tok_count, DH)


def project_kernel(n, local_ref, routed_ref, wl_ref, wr_ref, out_ref,
                   x, send, recv, send_sem, recv_sem):
    me = lax.axis_index("heads")
    tok_count, cols = out_ref.shape
    barrier = pltpu.get_barrier_semaphore()
    for k in range(1, n):
        pl.semaphore_signal(barrier, inc=1, device_id={"heads": lax.rem(me + k, n)},
                            device_id_type=MESH)
    for h in range(routed_ref.shape[0]):
        x[:, h * DH:(h + 1) * DH] = routed_ref[h]
    tile = min(512, cols)

    def product(owner, c):
        at = pl.ds(pl.multiple_of(owner * cols + c * tile, tile), tile)
        return dot(local_ref[...], wl_ref[:, at]) + dot(x[...], wr_ref[:, at])

    copies = []
    for k in range(1, n):
        owner = lax.rem(me + k, n)
        for c in range(cols // tile):
            send[k - 1, c] = product(owner, c).astype(jnp.bfloat16)
            if k == 1 and c == 0:
                pl.semaphore_wait(barrier, n - 1)
            copy = pltpu.make_async_remote_copy(
                src_ref=send.at[k - 1, c], dst_ref=recv.at[k - 1, c],
                send_sem=send_sem.at[k - 1, c], recv_sem=recv_sem.at[k - 1, c],
                device_id={"heads": owner}, device_id_type=MESH)
            copy.start()
            copies.append(copy)
    for c in range(cols // tile):
        total = product(me, c).astype(jnp.bfloat16).astype(jnp.float32)
        for k in range(1, n):
            copies[(k - 1) * (cols // tile) + c].wait_recv()
            total = total + recv[k - 1, c].astype(jnp.float32)
        out_ref[:, c * tile:(c + 1) * tile] = total.astype(jnp.bfloat16)
    for copy in copies:
        copy.wait_send()


def project(local_out, routed_out, wo_local, wo_routed):
    n = lax.axis_size("heads")
    tok_count = local_out.shape[0]
    cols = wo_local.shape[1] // n
    tile = min(512, cols)
    slots = (n - 1, cols // tile, tok_count, tile)
    return pl.pallas_call(
        functools.partial(project_kernel, n),
        out_shape=jax.ShapeDtypeStruct((tok_count, cols), jnp.bfloat16),
        in_specs=[vmem()] * 4,
        out_specs=vmem(),
        scratch_shapes=[
            pltpu.VMEM((tok_count, wo_routed.shape[0]), jnp.bfloat16),
            pltpu.VMEM(slots, jnp.bfloat16),
            pltpu.VMEM(slots, jnp.bfloat16),
            pltpu.SemaphoreType.DMA(slots[:2]),
            pltpu.SemaphoreType.DMA(slots[:2]),
        ],
        compiler_params=pltpu.CompilerParams(
            vmem_limit_bytes=VMEM_LIMIT, collective_id=0, has_side_effects=True),
    )(local_out, routed_out, wo_local, wo_routed)


def body(local_qkv, routed_qkv, clusters, wo_local, wo_routed):
    routed_out = routed_part(routed_qkv, clusters)
    local_out = window_part(local_qkv)
    return project(local_out, routed_out, wo_local, wo_routed)


def solution(mesh):
    return jax.shard_map(
        body,
        mesh=mesh,
        in_specs=(
            P(None, "seq", "heads"),
            P(None, "seq", "heads"),
            P("heads", "seq"),
            P("heads", None),
            P("heads", None),
        ),
        out_specs=P("seq", "heads"),
        check_vma=False,
    )
```

```python
import functools
import math

import jax
import jax.numpy as jnp
from jax import lax
from jax.experimental import pallas as pl
from jax.experimental.pallas import tpu as pltpu
from jax.sharding import PartitionSpec as P

DH = 128
WINDOW = 512
MASKED = -1e30
SCALE2 = math.log2(math.e) / math.sqrt(DH)
VMEM_LIMIT = 56 << 20

NT = (((1,), (1,)), ((), ()))
MESH = pl.DeviceIdType.MESH


def vmem():
    return pl.BlockSpec(memory_space=pltpu.VMEM)


def dot_nt(a, b):
    return lax.dot_general(a, b, NT, preferred_element_type=jnp.float32)


def dot(a, b):
    return jnp.dot(a, b, preferred_element_type=jnp.float32)


def window_kernel(first_ref, own_ref, prev_ref, out_ref):
    tok_count, width = out_ref.shape
    rows = min(256, tok_count)
    span = rows + WINDOW
    is_first = first_ref[0] == 0
    for i in range(tok_count // rows):
        r = lax.broadcasted_iota(jnp.int32, (rows, span), 0)
        c = lax.broadcasted_iota(jnp.int32, (rows, span), 1)
        from_prev = WINDOW - i * rows
        lowest = jnp.where(is_first, from_prev, 0)
        allowed = (c > r) & (c <= r + WINDOW) & (c >= lowest)
        for h in range(width // DH):
            cols = slice(h * DH, (h + 1) * DH)
            q = own_ref[0, i * rows:(i + 1) * rows, cols]
            k = jnp.concatenate(
                [prev_ref[0, i * rows:, cols], own_ref[1, :(i + 1) * rows, cols]], axis=0)
            v = jnp.concatenate(
                [prev_ref[1, i * rows:, cols], own_ref[2, :(i + 1) * rows, cols]], axis=0)
            s = jnp.where(allowed, dot_nt(q, k), MASKED)
            top = jnp.max(s, axis=-1, keepdims=True)
            p = jnp.exp2((s - top) * SCALE2)
            total = jnp.sum(p, axis=-1, keepdims=True)
            o = dot(p.astype(jnp.bfloat16), v) / total
            out_ref[i * rows:(i + 1) * rows, cols] = o.astype(jnp.bfloat16)


def window_part(local_qkv):
    tok_count = local_qkv.shape[1]
    width = local_qkv.shape[2]
    n = lax.axis_size("seq")
    prev = lax.ppermute(local_qkv[1:], "seq", [(i, i + 1) for i in range(n - 1)])
    where_at = lax.axis_index("seq").astype(jnp.int32).reshape(1)
    return pl.pallas_call(
        window_kernel,
        out_shape=jax.ShapeDtypeStruct((tok_count, width), jnp.bfloat16),
        in_specs=[pl.BlockSpec(memory_space=pltpu.SMEM), vmem(), vmem()],
        out_specs=vmem(),
        cost_estimate=pl.CostEstimate(
            flops=4 * tok_count * 768 * width, bytes_accessed=6 << 20, transcendentals=2 << 20),
        compiler_params=pltpu.CompilerParams(vmem_limit_bytes=VMEM_LIMIT),
    )(where_at, local_qkv, prev)


def flipped(me, t, n):
    out = 0
    bit = 1
    while bit < n:
        out = out + lax.rem(lax.div(me, bit) + lax.div(jnp.int32(t), bit), 2) * bit
        bit *= 2
    return out


def cluster_kernel(n, heads, qkv_ref, id_ref, out_ref, rq, kv, ck, cq, acc, top, total, done,
                   own_sem, q_sem, kv_sem, id_sem, pass_sem, back_sem):
    group = n // heads
    tok_count = out_ref.shape[1]
    rows = tok_count // group
    tile = min(256, tok_count)
    me = lax.axis_index("seq")
    head = lax.div(me, group)
    part = lax.rem(me, group)

    def rows_of(p):
        return pl.ds(pl.multiple_of(p * rows, rows), rows)

    def remote(src, dst, sem, index, device):
        return pltpu.make_async_remote_copy(
            src_ref=src, dst_ref=dst, send_sem=sem.at[(0,) + index], recv_sem=sem.at[(1,) + index],
            device_id={"seq": device}, device_id_type=MESH)

    def copies(t):
        d = flipped(me, t, n)
        h = pl.ds(pl.multiple_of(lax.div(d, group) * DH, DH), DH)
        p = rows_of(lax.rem(d, group))
        return (
            remote(id_ref.at[lax.div(d, group)], ck.at[me], id_sem, (t,), d),
            remote(qkv_ref.at[pl.ds(1, 2), p, h], kv.at[me, :, p], kv_sem, (t,), d),
            remote(qkv_ref.at[0, p, h], rq.at[me], q_sem, (t,), d),
        )

    def passed(u, g):
        src = kv.at[pl.ds(flipped(head, u, heads) * group, group), :, rows_of(part)]
        return remote(src, src, pass_sem, (u, g - 1), flipped(me, g, n))

    barrier = pltpu.get_barrier_semaphore()

    def greet(t, _):
        pl.semaphore_signal(barrier, inc=1, device_id={"seq": flipped(me, t, n)},
                            device_id_type=MESH)
        return 0

    lax.fori_loop(1, n, greet, 0)
    my_cols = pl.ds(pl.multiple_of(head * DH, DH), DH)
    own = (
        pltpu.make_async_copy(id_ref.at[head], ck.at[me], own_sem.at[0]),
        pltpu.make_async_copy(qkv_ref.at[pl.ds(1, 2), rows_of(part), my_cols],
                              kv.at[me, :, rows_of(part)], own_sem.at[1]),
        pltpu.make_async_copy(qkv_ref.at[0, rows_of(part), my_cols], rq.at[me], own_sem.at[2]),
    )
    for copy in own:
        copy.start()
    pl.semaphore_wait(barrier, n - 1)

    def send(t, _):
        for copy in copies(t):
            copy.start()
        return 0

    lax.fori_loop(1, n, send, 0)

    def update(qg, kg, c, r, diagonal):
        blocks = min(2, group)
        if diagonal and group == 2 and rows == tile:
            blocks = r + 1
        span = blocks * tok_count
        at = slice(r * tile, (r + 1) * tile)
        first = kg * group + c * 2
        per = tile // rows
        q = rq[pl.ds(qg * group + r * per, per)].reshape(tile, DH)
        k = kv[pl.ds(first, blocks), 0].reshape(span, DH)
        v = kv[pl.ds(first, blocks), 1].reshape(span, DH)
        ids = jnp.concatenate([ck[first + i] for i in range(blocks)], axis=1)
        allowed = cq[qg, at, :1] == ids.astype(jnp.float32)
        if diagonal:
            i = r * tile + lax.broadcasted_iota(jnp.int32, (tile, 1), 0)
            shift = rows.bit_length() - 1
            place = (i >> shift) * tok_count + part * rows + (i & (rows - 1))
            key = c * 2 * tok_count + lax.broadcasted_iota(jnp.int32, (1, span), 1)
            allowed = allowed & (key <= place)
        s = jnp.where(allowed, dot_nt(q, k), MASKED)
        old = top[qg, at]
        new = jnp.maximum(old, jnp.max(s, axis=-1, keepdims=True))
        fade = jnp.exp2((old - new) * SCALE2)
        p = jnp.exp2((s - new) * SCALE2)
        top[qg, at] = new
        total[qg, at] = fade * total[qg, at] + jnp.sum(p, axis=-1, keepdims=True)
        acc[qg, at] = fade * acc[qg, at] + dot(p.astype(jnp.bfloat16), v)

    def updates(qg, kg, diagonal):
        def chunk(c, _):
            for r in range(tok_count // tile):
                update(qg, kg, c, r, diagonal)
            return 0

        if group <= 2:
            chunk(0, 0)
        else:
            lax.fori_loop(0, group // 2, chunk, 0)

    def back(t):
        d = flipped(me, t, n)
        return remote(done.at[d], out_ref.at[head, rows_of(part)], back_sem, (t,), d)

    own_back = pltpu.make_async_copy(done.at[me], out_ref.at[head, rows_of(part)], own_sem.at[3])

    def finish(v):
        g = flipped(head, v, heads)
        o = (acc[g] / total[g]).astype(jnp.bfloat16)
        done[pl.ds(g * group, group)] = o.reshape(group, rows, DH)
        if v == 0:
            own_back.start()

        def give(t, _):
            back(t).start()
            return 0

        lax.fori_loop(max(v * group, 1), (v + 1) * group, give, 0)

    for u in range(heads):
        if u == 0:
            for copy in own:
                copy.wait()

        def arrive(t, _):
            for copy in copies(t):
                copy.wait_recv()
            return 0

        lax.fori_loop(max(u * group, 1), (u + 1) * group, arrive, 0)
        for g in range(1, group):
            passed(u, g).start()
        a = flipped(head, u, heads)

        def prepare(w, _):
            row = ck[a * group + w].astype(jnp.float32)
            column = jnp.transpose(jnp.broadcast_to(row, (128, tok_count)))
            done_rows = pl.ds(pl.multiple_of(w * rows, rows), rows)
            acc[a] = column
            cq[a, done_rows] = acc[a, rows_of(part)]
            return 0

        lax.fori_loop(0, group, prepare, 0)
        top[a] = jnp.full(top.shape[1:], MASKED, jnp.float32)
        total[a] = jnp.zeros(total.shape[1:], jnp.float32)
        acc[a] = jnp.zeros(acc.shape[1:], jnp.float32)
        for g in range(1, group):
            passed(u, g).wait_recv()
        updates(a, a, True)
        for v in reversed(range(u)):
            b = flipped(head, v, heads)
            updates(jnp.maximum(a, b), jnp.minimum(a, b), False)
            if u == heads - 1:
                finish(v)
    finish(heads - 1)

    def settle(t, _):
        for copy in copies(t):
            copy.wait_send()
        back(t).wait()
        return 0

    lax.fori_loop(1, n, settle, 0)
    own_back.wait()
    for u in range(heads):
        for g in range(1, group):
            passed(u, g).wait_send()


def routed_part(routed_qkv, clusters):
    tok_count = routed_qkv.shape[1]
    heads = clusters.shape[0]
    n = lax.axis_size("seq")
    group = n // heads
    rows = tok_count // group
    DMA = pltpu.SemaphoreType.DMA
    return pl.pallas_call(
        functools.partial(cluster_kernel, n, heads),
        out_shape=jax.ShapeDtypeStruct((heads, tok_count, DH), jnp.bfloat16),
        in_specs=[vmem()] * 2,
        out_specs=vmem(),
        scratch_shapes=[
            pltpu.VMEM((n, rows, DH), jnp.bfloat16),
            pltpu.VMEM((n, 2, tok_count, DH), jnp.bfloat16),
            pltpu.VMEM((n, 1, tok_count), jnp.int32),
            pltpu.VMEM((heads, tok_count, 128), jnp.float32),
            pltpu.VMEM((heads, tok_count, DH), jnp.float32),
            pltpu.VMEM((heads, tok_count, 1), jnp.float32),
            pltpu.VMEM((heads, tok_count, 1), jnp.float32),
            pltpu.VMEM((n, rows, DH), jnp.bfloat16),
            DMA((4,)), DMA((2, n)), DMA((2, n)), DMA((2, n)),
            DMA((2, heads, max(group - 1, 1))), DMA((2, n)),
        ],
        cost_estimate=pl.CostEstimate(
            flops=4 << 30, bytes_accessed=200 << 20, transcendentals=8 << 20),
        compiler_params=pltpu.CompilerParams(
            vmem_limit_bytes=VMEM_LIMIT, collective_id=1, has_side_effects=True),
    )(routed_qkv, clusters.reshape(heads, 1, tok_count))


def project_kernel(n, local_ref, routed_ref, wl_ref, wr_ref, out_ref,
                   x, send, recv, send_sem, recv_sem):
    me = lax.axis_index("heads")
    tok_count, cols = out_ref.shape
    barrier = pltpu.get_barrier_semaphore()
    for k in range(1, n):
        pl.semaphore_signal(barrier, inc=1, device_id={"heads": lax.rem(me + k, n)},
                            device_id_type=MESH)
    for h in range(routed_ref.shape[0]):
        x[:, h * DH:(h + 1) * DH] = routed_ref[h]
    tile = min(512, cols)

    def product(owner, c):
        at = pl.ds(pl.multiple_of(owner * cols + c * tile, tile), tile)
        return dot(local_ref[...], wl_ref[:, at]) + dot(x[...], wr_ref[:, at])

    copies = []
    for k in range(1, n):
        owner = lax.rem(me + k, n)
        for c in range(cols // tile):
            send[k - 1, c] = product(owner, c).astype(jnp.bfloat16)
            if k == 1 and c == 0:
                pl.semaphore_wait(barrier, n - 1)
            copy = pltpu.make_async_remote_copy(
                src_ref=send.at[k - 1, c], dst_ref=recv.at[k - 1, c],
                send_sem=send_sem.at[k - 1, c], recv_sem=recv_sem.at[k - 1, c],
                device_id={"heads": owner}, device_id_type=MESH)
            copy.start()
            copies.append(copy)
    for c in range(cols // tile):
        total = product(me, c).astype(jnp.bfloat16).astype(jnp.float32)
        for k in range(1, n):
            copies[(k - 1) * (cols // tile) + c].wait_recv()
            total = total + recv[k - 1, c].astype(jnp.float32)
        out_ref[:, c * tile:(c + 1) * tile] = total.astype(jnp.bfloat16)
    for copy in copies:
        copy.wait_send()


def project(local_out, routed_out, wo_local, wo_routed):
    n = lax.axis_size("heads")
    tok_count = local_out.shape[0]
    cols = wo_local.shape[1] // n
    tile = min(512, cols)
    slots = (n - 1, cols // tile, tok_count, tile)
    return pl.pallas_call(
        functools.partial(project_kernel, n),
        out_shape=jax.ShapeDtypeStruct((tok_count, cols), jnp.bfloat16),
        in_specs=[vmem()] * 4,
        out_specs=vmem(),
        scratch_shapes=[
            pltpu.VMEM((tok_count, wo_routed.shape[0]), jnp.bfloat16),
            pltpu.VMEM(slots, jnp.bfloat16),
            pltpu.VMEM(slots, jnp.bfloat16),
            pltpu.SemaphoreType.DMA(slots[:2]),
            pltpu.SemaphoreType.DMA(slots[:2]),
        ],
        compiler_params=pltpu.CompilerParams(
            vmem_limit_bytes=VMEM_LIMIT, collective_id=0, has_side_effects=True),
    )(local_out, routed_out, wo_local, wo_routed)


def body(local_qkv, routed_qkv, clusters, wo_local, wo_routed):
    routed_out = routed_part(routed_qkv, clusters)
    local_out = window_part(local_qkv)
    return project(local_out, routed_out, wo_local, wo_routed)


def solution(mesh):
    return jax.shard_map(
        body,
        mesh=mesh,
        in_specs=(
            P(None, "seq", "heads"),
            P(None, "seq", "heads"),
            P("heads", "seq"),
            P("heads", None),
            P("heads", None),
        ),
        out_specs=P("seq", "heads"),
        check_vma=False,
    )
```

```python
import functools
import math

import jax
import jax.numpy as jnp
from jax import lax
from jax.experimental import pallas as pl
from jax.experimental.pallas import tpu as pltpu
from jax.sharding import PartitionSpec as P

DH = 128
WINDOW = 512
MASKED = -1e30
SCALE2 = math.log2(math.e) / math.sqrt(DH)
VMEM_LIMIT = 56 << 20

NT = (((1,), (1,)), ((), ()))
MESH = pl.DeviceIdType.MESH


def vmem():
    return pl.BlockSpec(memory_space=pltpu.VMEM)


def dot_nt(a, b):
    return lax.dot_general(a, b, NT, preferred_element_type=jnp.float32)


def dot(a, b):
    return jnp.dot(a, b, preferred_element_type=jnp.float32)


def window_heads(is_first, own_ref, prev_ref, out_ref):
    tok_count, width = out_ref.shape
    rows = min(256, tok_count)
    span = rows + WINDOW
    for i in range(tok_count // rows):
        r = lax.broadcasted_iota(jnp.int32, (rows, span), 0)
        c = lax.broadcasted_iota(jnp.int32, (rows, span), 1)
        from_prev = WINDOW - i * rows
        lowest = jnp.where(is_first, from_prev, 0)
        allowed = (c > r) & (c <= r + WINDOW) & (c >= lowest)
        for h in range(width // DH):
            cols = slice(h * DH, (h + 1) * DH)
            q = own_ref[0, i * rows:(i + 1) * rows, cols]
            k = jnp.concatenate(
                [prev_ref[0, i * rows:, cols], own_ref[1, :(i + 1) * rows, cols]], axis=0)
            v = jnp.concatenate(
                [prev_ref[1, i * rows:, cols], own_ref[2, :(i + 1) * rows, cols]], axis=0)
            s = jnp.where(allowed, dot_nt(q, k), MASKED)
            top = jnp.max(s, axis=-1, keepdims=True)
            p = jnp.exp2((s - top) * SCALE2)
            total = jnp.sum(p, axis=-1, keepdims=True)
            o = dot(p.astype(jnp.bfloat16), v) / total
            out_ref[i * rows:(i + 1) * rows, cols] = o.astype(jnp.bfloat16)


def flipped(me, t, n):
    out = 0
    bit = 1
    while bit < n:
        out = out + lax.rem(lax.div(me, bit) + lax.div(jnp.int32(t), bit), 2) * bit
        bit *= 2
    return out


def attention_kernel(n, heads, qkv_ref, id_ref, local_ref, out_ref, local_out_ref, prev, rq, kv, ck, cq, acc, top, total, done,
                   own_sem, q_sem, kv_sem, id_sem, pass_sem, back_sem, prev_sem):
    group = n // heads
    tok_count = out_ref.shape[1]
    rows = tok_count // group
    tile = min(256, tok_count)
    me = lax.axis_index("seq")
    head = lax.div(me, group)
    part = lax.rem(me, group)

    def rows_of(p):
        return pl.ds(pl.multiple_of(p * rows, rows), rows)

    def remote(src, dst, sem, index, device):
        return pltpu.make_async_remote_copy(
            src_ref=src, dst_ref=dst, send_sem=sem.at[(0,) + index], recv_sem=sem.at[(1,) + index],
            device_id={"seq": device}, device_id_type=MESH)

    def copies(t):
        d = flipped(me, t, n)
        h = pl.ds(pl.multiple_of(lax.div(d, group) * DH, DH), DH)
        p = rows_of(lax.rem(d, group))
        return (
            remote(id_ref.at[lax.div(d, group)], ck.at[me], id_sem, (t,), d),
            remote(qkv_ref.at[pl.ds(1, 2), p, h], kv.at[me, :, p], kv_sem, (t,), d),
            remote(qkv_ref.at[0, p, h], rq.at[me], q_sem, (t,), d),
        )

    def passed(u, g):
        src = kv.at[pl.ds(flipped(head, u, heads) * group, group), :, rows_of(part)]
        return remote(src, src, pass_sem, (u, g - 1), flipped(me, g, n))

    barrier = pltpu.get_barrier_semaphore()

    def greet(t, _):
        pl.semaphore_signal(barrier, inc=1, device_id={"seq": flipped(me, t, n)},
                            device_id_type=MESH)
        return 0

    lax.fori_loop(1, n, greet, 0)
    my_cols = pl.ds(pl.multiple_of(head * DH, DH), DH)
    own = (
        pltpu.make_async_copy(id_ref.at[head], ck.at[me], own_sem.at[0]),
        pltpu.make_async_copy(qkv_ref.at[pl.ds(1, 2), rows_of(part), my_cols],
                              kv.at[me, :, rows_of(part)], own_sem.at[1]),
        pltpu.make_async_copy(qkv_ref.at[0, rows_of(part), my_cols], rq.at[me], own_sem.at[2]),
    )
    for copy in own:
        copy.start()
    pl.semaphore_wait(barrier, n - 1)

    def send(t, _):
        for copy in copies(t):
            copy.start()
        return 0

    lax.fori_loop(1, n, send, 0)
    prev_copy = remote(local_ref.at[pl.ds(1, 2)], prev, prev_sem, (), lax.rem(me + 1, n))

    @pl.when(me < n - 1)
    def _():
        prev_copy.start()

    @pl.when(me == 0)
    def _():
        prev[...] = jnp.zeros_like(prev)

    def update(qg, kg, c, r, diagonal):
        blocks = min(2, group)
        if diagonal and group == 2 and rows == tile:
            blocks = r + 1
        span = blocks * tok_count
        at = slice(r * tile, (r + 1) * tile)
        first = kg * group + c * 2
        per = tile // rows
        q = rq[pl.ds(qg * group + r * per, per)].reshape(tile, DH)
        k = kv[pl.ds(first, blocks), 0].reshape(span, DH)
        v = kv[pl.ds(first, blocks), 1].reshape(span, DH)
        ids = jnp.concatenate([ck[first + i] for i in range(blocks)], axis=1)
        allowed = cq[qg, at, :1] == ids.astype(jnp.float32)
        if diagonal:
            i = r * tile + lax.broadcasted_iota(jnp.int32, (tile, 1), 0)
            shift = rows.bit_length() - 1
            place = (i >> shift) * tok_count + part * rows + (i & (rows - 1))
            key = c * 2 * tok_count + lax.broadcasted_iota(jnp.int32, (1, span), 1)
            allowed = allowed & (key <= place)
        s = jnp.where(allowed, dot_nt(q, k), MASKED)
        old = top[qg, at]
        new = jnp.maximum(old, jnp.max(s, axis=-1, keepdims=True))
        fade = jnp.exp2((old - new) * SCALE2)
        p = jnp.exp2((s - new) * SCALE2)
        top[qg, at] = new
        total[qg, at] = fade * total[qg, at] + jnp.sum(p, axis=-1, keepdims=True)
        acc[qg, at] = fade * acc[qg, at] + dot(p.astype(jnp.bfloat16), v)

    def updates(qg, kg, diagonal):
        def chunk(c, _):
            for r in range(tok_count // tile):
                update(qg, kg, c, r, diagonal)
            return 0

        if group <= 2:
            chunk(0, 0)
        else:
            lax.fori_loop(0, group // 2, chunk, 0)

    def back(t):
        d = flipped(me, t, n)
        return remote(done.at[d], out_ref.at[head, rows_of(part)], back_sem, (t,), d)

    own_back = pltpu.make_async_copy(done.at[me], out_ref.at[head, rows_of(part)], own_sem.at[3])

    def finish(v):
        g = flipped(head, v, heads)
        o = (acc[g] / total[g]).astype(jnp.bfloat16)
        done[pl.ds(g * group, group)] = o.reshape(group, rows, DH)
        if v == 0:
            own_back.start()

        def give(t, _):
            back(t).start()
            return 0

        lax.fori_loop(max(v * group, 1), (v + 1) * group, give, 0)

    for u in range(heads):
        if u == 0:
            for copy in own:
                copy.wait()

        def arrive(t, _):
            for copy in copies(t):
                copy.wait_recv()
            return 0

        lax.fori_loop(max(u * group, 1), (u + 1) * group, arrive, 0)
        for g in range(1, group):
            passed(u, g).start()
        a = flipped(head, u, heads)

        def prepare(w, _):
            row = ck[a * group + w].astype(jnp.float32)
            column = jnp.transpose(jnp.broadcast_to(row, (128, tok_count)))
            done_rows = pl.ds(pl.multiple_of(w * rows, rows), rows)
            acc[a] = column
            cq[a, done_rows] = acc[a, rows_of(part)]
            return 0

        lax.fori_loop(0, group, prepare, 0)
        top[a] = jnp.full(top.shape[1:], MASKED, jnp.float32)
        total[a] = jnp.zeros(total.shape[1:], jnp.float32)
        acc[a] = jnp.zeros(acc.shape[1:], jnp.float32)
        for g in range(1, group):
            passed(u, g).wait_recv()
        updates(a, a, True)
        for v in reversed(range(u)):
            b = flipped(head, v, heads)
            updates(jnp.maximum(a, b), jnp.minimum(a, b), False)
            if u == heads - 1:
                finish(v)
    finish(heads - 1)

    @pl.when(me > 0)
    def _():
        prev_copy.wait_recv()

    window_heads(me == 0, local_ref, prev, local_out_ref)

    @pl.when(me < n - 1)
    def _():
        prev_copy.wait_send()

    def settle(t, _):
        for copy in copies(t):
            copy.wait_send()
        back(t).wait()
        return 0

    lax.fori_loop(1, n, settle, 0)
    own_back.wait()
    for u in range(heads):
        for g in range(1, group):
            passed(u, g).wait_send()


def attention(local_qkv, routed_qkv, clusters):
    tok_count = routed_qkv.shape[1]
    heads = clusters.shape[0]
    n = lax.axis_size("seq")
    group = n // heads
    rows = tok_count // group
    DMA = pltpu.SemaphoreType.DMA
    return pl.pallas_call(
        functools.partial(attention_kernel, n, heads),
        out_shape=(
            jax.ShapeDtypeStruct((heads, tok_count, DH), jnp.bfloat16),
            jax.ShapeDtypeStruct(local_qkv.shape[1:], jnp.bfloat16),
        ),
        in_specs=[vmem()] * 3,
        out_specs=(vmem(), vmem()),
        scratch_shapes=[
            pltpu.VMEM((2,) + local_qkv.shape[1:], jnp.bfloat16),
            pltpu.VMEM((n, rows, DH), jnp.bfloat16),
            pltpu.VMEM((n, 2, tok_count, DH), jnp.bfloat16),
            pltpu.VMEM((n, 1, tok_count), jnp.int32),
            pltpu.VMEM((heads, tok_count, 128), jnp.float32),
            pltpu.VMEM((heads, tok_count, DH), jnp.float32),
            pltpu.VMEM((heads, tok_count, 1), jnp.float32),
            pltpu.VMEM((heads, tok_count, 1), jnp.float32),
            pltpu.VMEM((n, rows, DH), jnp.bfloat16),
            DMA((4,)), DMA((2, n)), DMA((2, n)), DMA((2, n)),
            DMA((2, heads, max(group - 1, 1))), DMA((2, n)), DMA((2,)),
        ],
        cost_estimate=pl.CostEstimate(
            flops=4 << 30, bytes_accessed=200 << 20, transcendentals=8 << 20),
        compiler_params=pltpu.CompilerParams(
            vmem_limit_bytes=VMEM_LIMIT, collective_id=1, has_side_effects=True),
    )(routed_qkv, clusters.reshape(heads, 1, tok_count), local_qkv)


def project_kernel(local_ref, routed_ref, wl_ref, wr_ref, out_ref,
                   x, send, recv, send_sem, recv_sem):
    me = lax.axis_index("heads")
    tok_count, cols = out_ref.shape
    pieces = send.shape[1]
    tile = cols // pieces
    across = (me + 1 - 2 * lax.rem(me, 2), lax.rem(me + 2, 4))
    corner = lax.rem(across[0] + 2, 4)
    barrier = pltpu.get_barrier_semaphore()
    for device in across:
        pl.semaphore_signal(barrier, inc=1, device_id={"heads": device}, device_id_type=MESH)
    for h in range(routed_ref.shape[0]):
        x[:, h * DH:(h + 1) * DH] = routed_ref[h]

    def product(owner, c):
        at = pl.ds(pl.multiple_of(owner * cols + c * tile, tile), tile)
        return dot(local_ref[...], wl_ref[:, at]) + dot(x[...], wr_ref[:, at])

    def hand(kind, c, value, device):
        send[kind, c] = value.astype(jnp.bfloat16)
        return pltpu.make_async_remote_copy(
            src_ref=send.at[kind, c], dst_ref=recv.at[kind, c],
            send_sem=send_sem.at[kind, c], recv_sem=recv_sem.at[kind, c],
            device_id={"heads": device}, device_id_type=MESH)

    order = [c + half * (pieces // 2) for c in range(pieces // 2) for half in range(2)]
    way = [c // (pieces // 2) for c in range(pieces)]
    copies = {}
    for kind in range(2):
        for c in order:
            device = across[way[c]]
            copies[kind, c] = hand(kind, c, product(device if kind else corner, c), device)
            if not kind and c == order[0]:
                pl.semaphore_wait(barrier, 2)
            copies[kind, c].start()
    for c in order:
        device = across[1 - way[c]]
        value = product(device, c)
        copies[0, c].wait_recv()
        copies[2, c] = hand(2, c, value + recv[0, c].astype(jnp.float32), device)
        copies[2, c].start()
    for c in order:
        value = product(me, c)
        copies[1, c].wait_recv()
        value = value + recv[1, c].astype(jnp.float32)
        copies[2, c].wait_recv()
        value = value + recv[2, c].astype(jnp.float32)
        out_ref[:, c * tile:(c + 1) * tile] = value.astype(jnp.bfloat16)
    for copy in copies.values():
        copy.wait_send()


def project(local_out, routed_out, wo_local, wo_routed):
    tok_count = local_out.shape[0]
    cols = wo_local.shape[1] // lax.axis_size("heads")
    pieces = 4
    slots = (3, pieces, tok_count, cols // pieces)
    return pl.pallas_call(
        project_kernel,
        out_shape=jax.ShapeDtypeStruct((tok_count, cols), jnp.bfloat16),
        in_specs=[vmem()] * 4,
        out_specs=vmem(),
        scratch_shapes=[
            pltpu.VMEM((tok_count, wo_routed.shape[0]), jnp.bfloat16),
            pltpu.VMEM(slots, jnp.bfloat16),
            pltpu.VMEM(slots, jnp.bfloat16),
            pltpu.SemaphoreType.DMA(slots[:2]),
            pltpu.SemaphoreType.DMA(slots[:2]),
        ],
        compiler_params=pltpu.CompilerParams(
            vmem_limit_bytes=VMEM_LIMIT, collective_id=0, has_side_effects=True),
    )(local_out, routed_out, wo_local, wo_routed)


def body(local_qkv, routed_qkv, clusters, wo_local, wo_routed):
    routed_out, local_out = attention(local_qkv, routed_qkv, clusters)
    return project(local_out, routed_out, wo_local, wo_routed)


def solution(mesh):
    return jax.shard_map(
        body,
        mesh=mesh,
        in_specs=(
            P(None, "seq", "heads"),
            P(None, "seq", "heads"),
            P("heads", "seq"),
            P("heads", None),
            P("heads", None),
        ),
        out_specs=P("seq", "heads"),
        check_vma=False,
    )
```

```python
import functools
import math

import jax
import jax.numpy as jnp
from jax import lax
from jax.experimental import pallas as pl
from jax.experimental.pallas import tpu as pltpu
from jax.sharding import PartitionSpec as P

DH = 128
WINDOW = 512
MASKED = -1e30
SCALE2 = math.log2(math.e) / math.sqrt(DH)
VMEM_LIMIT = 56 << 20

NT = (((1,), (1,)), ((), ()))
MESH = pl.DeviceIdType.MESH


def vmem():
    return pl.BlockSpec(memory_space=pltpu.VMEM)


def dot_nt(a, b):
    return lax.dot_general(a, b, NT, preferred_element_type=jnp.float32)


def dot(a, b):
    return jnp.dot(a, b, preferred_element_type=jnp.float32)


def window_heads(is_first, own_ref, prev_ref, out_ref):
    tok_count, width = out_ref.shape
    rows = min(256, tok_count)
    span = rows + WINDOW
    for i in range(tok_count // rows):
        r = lax.broadcasted_iota(jnp.int32, (rows, span), 0)
        c = lax.broadcasted_iota(jnp.int32, (rows, span), 1)
        from_prev = WINDOW - i * rows
        lowest = jnp.where(is_first, from_prev, 0)
        allowed = (c > r) & (c <= r + WINDOW) & (c >= lowest)
        for h in range(width // DH):
            cols = slice(h * DH, (h + 1) * DH)
            q = own_ref[0, i * rows:(i + 1) * rows, cols]
            k = jnp.concatenate(
                [prev_ref[0, i * rows:, cols], own_ref[1, :(i + 1) * rows, cols]], axis=0)
            v = jnp.concatenate(
                [prev_ref[1, i * rows:, cols], own_ref[2, :(i + 1) * rows, cols]], axis=0)
            s = jnp.where(allowed, dot_nt(q, k), MASKED)
            top = jnp.max(s, axis=-1, keepdims=True)
            p = jnp.exp2((s - top) * SCALE2)
            total = jnp.sum(p, axis=-1, keepdims=True)
            o = dot(p.astype(jnp.bfloat16), v) / total
            out_ref[i * rows:(i + 1) * rows, cols] = o.astype(jnp.bfloat16)


def flipped(me, t, n):
    out = 0
    bit = 1
    while bit < n:
        out = out + lax.rem(lax.div(me, bit) + lax.div(jnp.int32(t), bit), 2) * bit
        bit *= 2
    return out


def layer_kernel(n, heads, qkv_ref, id_ref, local_ref, wl_any, wr_any, out_ref, prev, rq, kv, ck, cq, acc, top, total, done,
                   own_sem, q_sem, kv_sem, id_sem, pass_sem, back_sem, prev_sem,
                 local_out, x, wl, wr, tiles_out, tiles_in, out_sem, in_sem, w_sem):
    group = n // heads
    tok_count = x.shape[0]
    rows = tok_count // group
    tile = min(256, tok_count)
    me = lax.axis_index("seq")
    head = lax.div(me, group)
    part = lax.rem(me, group)

    def rows_of(p):
        return pl.ds(pl.multiple_of(p * rows, rows), rows)

    def remote(src, dst, sem, index, device):
        return pltpu.make_async_remote_copy(
            src_ref=src, dst_ref=dst, send_sem=sem.at[(0,) + index], recv_sem=sem.at[(1,) + index],
            device_id={"seq": device}, device_id_type=MESH)

    def copies(t):
        d = flipped(me, t, n)
        h = pl.ds(pl.multiple_of(lax.div(d, group) * DH, DH), DH)
        p = rows_of(lax.rem(d, group))
        return (
            remote(id_ref.at[lax.div(d, group)], ck.at[me], id_sem, (t,), d),
            remote(qkv_ref.at[pl.ds(1, 2), p, h], kv.at[me, :, p], kv_sem, (t,), d),
            remote(qkv_ref.at[0, p, h], rq.at[me], q_sem, (t,), d),
        )

    def passed(u, g):
        src = kv.at[pl.ds(flipped(head, u, heads) * group, group), :, rows_of(part)]
        return remote(src, src, pass_sem, (u, g - 1), flipped(me, g, n))

    barrier = pltpu.get_barrier_semaphore()

    def greet(t, _):
        pl.semaphore_signal(barrier, inc=1, device_id={"seq": flipped(me, t, n)},
                            device_id_type=MESH)
        return 0

    lax.fori_loop(1, n, greet, 0)
    place = lax.axis_index("heads")
    across = (place + 1 - 2 * lax.rem(place, 2), lax.rem(place + 2, 4))
    for device in across:
        pl.semaphore_signal(barrier, inc=1, device_id={"heads": device}, device_id_type=MESH)
    weights = (
        pltpu.make_async_copy(wl_any, wl, w_sem.at[0]),
        pltpu.make_async_copy(wr_any, wr, w_sem.at[1]),
    )
    my_cols = pl.ds(pl.multiple_of(head * DH, DH), DH)
    own = (
        pltpu.make_async_copy(id_ref.at[head], ck.at[me], own_sem.at[0]),
        pltpu.make_async_copy(qkv_ref.at[pl.ds(1, 2), rows_of(part), my_cols],
                              kv.at[me, :, rows_of(part)], own_sem.at[1]),
        pltpu.make_async_copy(qkv_ref.at[0, rows_of(part), my_cols], rq.at[me], own_sem.at[2]),
    )
    for copy in own:
        copy.start()
    pl.semaphore_wait(barrier, n - 1 + len(across))

    def send(t, _):
        for copy in copies(t):
            copy.start()
        return 0

    lax.fori_loop(1, n, send, 0)
    for copy in weights:
        copy.start()
    prev_copy = remote(local_ref.at[pl.ds(1, 2)], prev, prev_sem, (), lax.rem(me + 1, n))

    @pl.when(me < n - 1)
    def _():
        prev_copy.start()

    @pl.when(me == 0)
    def _():
        prev[...] = jnp.zeros_like(prev)

    def update(qg, kg, c, r, diagonal):
        blocks = min(2, group)
        if diagonal and group == 2 and rows == tile:
            blocks = r + 1
        span = blocks * tok_count
        at = slice(r * tile, (r + 1) * tile)
        first = kg * group + c * 2
        per = tile // rows
        q = rq[pl.ds(qg * group + r * per, per)].reshape(tile, DH)
        k = kv[pl.ds(first, blocks), 0].reshape(span, DH)
        v = kv[pl.ds(first, blocks), 1].reshape(span, DH)
        ids = jnp.concatenate([ck[first + i] for i in range(blocks)], axis=1)
        allowed = cq[qg, at, :1] == ids.astype(jnp.float32)
        if diagonal:
            i = r * tile + lax.broadcasted_iota(jnp.int32, (tile, 1), 0)
            shift = rows.bit_length() - 1
            place = (i >> shift) * tok_count + part * rows + (i & (rows - 1))
            key = c * 2 * tok_count + lax.broadcasted_iota(jnp.int32, (1, span), 1)
            allowed = allowed & (key <= place)
        s = jnp.where(allowed, dot_nt(q, k), MASKED)
        old = top[qg, at]
        new = jnp.maximum(old, jnp.max(s, axis=-1, keepdims=True))
        fade = jnp.exp2((old - new) * SCALE2)
        p = jnp.exp2((s - new) * SCALE2)
        top[qg, at] = new
        total[qg, at] = fade * total[qg, at] + jnp.sum(p, axis=-1, keepdims=True)
        acc[qg, at] = fade * acc[qg, at] + dot(p.astype(jnp.bfloat16), v)

    def updates(qg, kg, diagonal):
        def chunk(c, _):
            for r in range(tok_count // tile):
                update(qg, kg, c, r, diagonal)
            return 0

        if group <= 2:
            chunk(0, 0)
        else:
            lax.fori_loop(0, group // 2, chunk, 0)

    def back(t):
        d = flipped(me, t, n)
        return remote(done.at[d], x.at[rows_of(part), my_cols], back_sem, (t,), d)

    own_back = pltpu.make_async_copy(done.at[me], x.at[rows_of(part), my_cols], own_sem.at[3])

    def finish(v):
        g = flipped(head, v, heads)
        o = (acc[g] / total[g]).astype(jnp.bfloat16)
        done[pl.ds(g * group, group)] = o.reshape(group, rows, DH)
        if v == 0:
            own_back.start()

        def give(t, _):
            back(t).start()
            return 0

        lax.fori_loop(max(v * group, 1), (v + 1) * group, give, 0)

    for u in range(heads):
        if u == 0:
            for copy in own:
                copy.wait()

        def arrive(t, _):
            for copy in copies(t):
                copy.wait_recv()
            return 0

        lax.fori_loop(max(u * group, 1), (u + 1) * group, arrive, 0)
        for g in range(1, group):
            passed(u, g).start()
        a = flipped(head, u, heads)

        def prepare(w, _):
            row = ck[a * group + w].astype(jnp.float32)
            column = jnp.transpose(jnp.broadcast_to(row, (128, tok_count)))
            done_rows = pl.ds(pl.multiple_of(w * rows, rows), rows)
            acc[a] = column
            cq[a, done_rows] = acc[a, rows_of(part)]
            return 0

        lax.fori_loop(0, group, prepare, 0)
        top[a] = jnp.full(top.shape[1:], MASKED, jnp.float32)
        total[a] = jnp.zeros(total.shape[1:], jnp.float32)
        acc[a] = jnp.zeros(acc.shape[1:], jnp.float32)
        for g in range(1, group):
            passed(u, g).wait_recv()
        updates(a, a, True)
        for v in reversed(range(u)):
            b = flipped(head, v, heads)
            updates(jnp.maximum(a, b), jnp.minimum(a, b), False)
            if u == heads - 1:
                finish(v)
    finish(heads - 1)

    @pl.when(me > 0)
    def _():
        prev_copy.wait_recv()

    window_heads(me == 0, local_ref, prev, local_out)

    @pl.when(me < n - 1)
    def _():
        prev_copy.wait_send()

    def settle(t, _):
        for copy in copies(t):
            copy.wait_send()
        back(t).wait()
        return 0

    lax.fori_loop(1, n, settle, 0)
    own_back.wait()
    for u in range(heads):
        for g in range(1, group):
            passed(u, g).wait_send()
    for copy in weights:
        copy.wait()
    project(place, across, local_out, x, wl, wr, out_ref, tiles_out, tiles_in, out_sem, in_sem)


def project(me, across, local_ref, x, wl_ref, wr_ref, out_ref, send, recv, send_sem, recv_sem):
    cols = out_ref.shape[1]
    pieces = send.shape[1]
    tile = cols // pieces
    corner = lax.rem(across[0] + 2, 4)

    def product(owner, c):
        at = pl.ds(pl.multiple_of(owner * cols + c * tile, tile), tile)
        return dot(local_ref[...], wl_ref[:, at]) + dot(x[...], wr_ref[:, at])

    def hand(kind, c, value, device):
        send[kind, c] = value.astype(jnp.bfloat16)
        return pltpu.make_async_remote_copy(
            src_ref=send.at[kind, c], dst_ref=recv.at[kind, c],
            send_sem=send_sem.at[kind, c], recv_sem=recv_sem.at[kind, c],
            device_id={"heads": device}, device_id_type=MESH)

    order = [c + half * (pieces // 2) for c in range(pieces // 2) for half in range(2)]
    way = [c // (pieces // 2) for c in range(pieces)]
    copies = {}
    for kind in range(2):
        for c in order:
            device = across[way[c]]
            copies[kind, c] = hand(kind, c, product(device if kind else corner, c), device)
            copies[kind, c].start()
    for c in order:
        device = across[1 - way[c]]
        value = product(device, c)
        copies[0, c].wait_recv()
        copies[2, c] = hand(2, c, value + recv[0, c].astype(jnp.float32), device)
        copies[2, c].start()
    for c in order:
        value = product(me, c)
        copies[1, c].wait_recv()
        value = value + recv[1, c].astype(jnp.float32)
        copies[2, c].wait_recv()
        value = value + recv[2, c].astype(jnp.float32)
        out_ref[:, c * tile:(c + 1) * tile] = value.astype(jnp.bfloat16)
    for copy in copies.values():
        copy.wait_send()


def body(local_qkv, routed_qkv, clusters, wo_local, wo_routed):
    tok_count = routed_qkv.shape[1]
    heads = clusters.shape[0]
    n = lax.axis_size("seq")
    group = n // heads
    rows = tok_count // group
    cols = wo_local.shape[1] // lax.axis_size("heads")
    slots = (3, 4, tok_count, cols // 4)
    DMA = pltpu.SemaphoreType.DMA
    return pl.pallas_call(
        functools.partial(layer_kernel, n, heads),
        out_shape=jax.ShapeDtypeStruct((tok_count, cols), jnp.bfloat16),
        in_specs=[vmem()] * 3 + [pl.BlockSpec(memory_space=pl.ANY)] * 2,
        out_specs=vmem(),
        scratch_shapes=[
            pltpu.VMEM((2,) + local_qkv.shape[1:], jnp.bfloat16),
            pltpu.VMEM((n, rows, DH), jnp.bfloat16),
            pltpu.VMEM((n, 2, tok_count, DH), jnp.bfloat16),
            pltpu.VMEM((n, 1, tok_count), jnp.int32),
            pltpu.VMEM((heads, tok_count, 128), jnp.float32),
            pltpu.VMEM((heads, tok_count, DH), jnp.float32),
            pltpu.VMEM((heads, tok_count, 1), jnp.float32),
            pltpu.VMEM((heads, tok_count, 1), jnp.float32),
            pltpu.VMEM((n, rows, DH), jnp.bfloat16),
            DMA((4,)), DMA((2, n)), DMA((2, n)), DMA((2, n)),
            DMA((2, heads, max(group - 1, 1))), DMA((2, n)), DMA((2,)),
            pltpu.VMEM(local_qkv.shape[1:], jnp.bfloat16),
            pltpu.VMEM((tok_count, heads * DH), jnp.bfloat16),
            pltpu.VMEM(wo_local.shape, jnp.bfloat16),
            pltpu.VMEM(wo_routed.shape, jnp.bfloat16),
            pltpu.VMEM(slots, jnp.bfloat16),
            pltpu.VMEM(slots, jnp.bfloat16),
            DMA(slots[:2]), DMA(slots[:2]), DMA((2,)),
        ],
        cost_estimate=pl.CostEstimate(
            flops=4 << 30, bytes_accessed=200 << 20, transcendentals=8 << 20),
        compiler_params=pltpu.CompilerParams(
            vmem_limit_bytes=VMEM_LIMIT, collective_id=0, has_side_effects=True),
    )(routed_qkv, clusters.reshape(heads, 1, tok_count), local_qkv, wo_local, wo_routed)


def solution(mesh):
    return jax.shard_map(
        body,
        mesh=mesh,
        in_specs=(
            P(None, "seq", "heads"),
            P(None, "seq", "heads"),
            P("heads", "seq"),
            P("heads", None),
            P("heads", None),
        ),
        out_specs=P("seq", "heads"),
        check_vma=False,
    )
```
